128 devices in a mesh: clip: 16 (over y, x), feat: 8 (over z, core).
Axes of the slice: x: 4, y: 4, z: 4, core: 2. Of those that a mesh axis runs over, the one named last changes fastest.
Arguments:
- features: float32 [12288, 22528], P('clip', 'feat'), may hold values from -20 to 20
- weights: float32 [400, 22528], P(None, 'feat'), may hold values from -0.02665009 to 0.02665009
- labels: int32 [12288], P('clip'), may hold values from 0 to 399
Outputs:
- new_weights: float32 [400, 22528], P(None, 'feat')
- residual: float32 [400, 22528], P(None, 'feat')
The draws below stay inside these ranges and needn't reach their ends.
All inputs are finite; a program needn't handle non-finite values.
Results may differ from the reference program's by a relative error of at most 0.0003.
Values sent between devices are 32-bit elements; how exact they have to be, the bound alone decides.
A program may use at most 128 MiB of HBM per device.

```python
import math
import jax
import jax.numpy as jnp
from jax import lax

FEATS = 22528
CLASSES = 400
ITERS = 2
ROWS = 12288


def shared_weights(key):
    noise = jax.random.normal(jax.random.fold_in(key, 11), (CLASSES, FEATS), jnp.float32)
    return jnp.clip(noise, -4.0, 4.0) / math.sqrt(FEATS)


def draw_weights(key, part):
    return shared_weights(key)


def draw_features(key, part):
    keyset = jax.random.split(jax.random.fold_in(key, 23), 1)
    noise = jnp.clip(jax.random.normal(keyset[0], (ROWS, FEATS), jnp.float32), -5.0, 5.0)
    return jnp.clip(noise, -20.0, 20.0)


def place_ends(values, key, smallest, high):
    shape = values.shape
    spot = [jax.random.randint(jax.random.fold_in(key, axis), (), 0, shape[axis]) for axis in range(len(shape))]
    values = values.at[tuple(spot)].set(smallest)
    longest = shape.index(max(shape))
    spot[longest] = (spot[longest] + 1) % shape[longest]
    return values.at[tuple(spot)].set(high)


def setup_inputs(seed: int = 0) -> dict:
    key_list = jax.random.split(jax.random.key(seed), 4)
    return {
        "features": draw_features(jax.random.fold_in(key_list[3], 71), 0),
        "weights": draw_weights(jax.random.fold_in(key_list[3], 71), 0),
        "labels": place_ends(jax.random.randint(key_list[2], (ROWS,), 0, CLASSES), jax.random.fold_in(key_list[2], 1), 0, CLASSES - 1).astype(jnp.int32),
    }


damping = 0.01


def reference(features, weights, labels):
    highest = lax.Precision.HIGHEST
    logits = jnp.dot(features, weights.T, precision=highest, preferred_element_type=jnp.float32)
    probs = jax.nn.softmax(logits, axis=1)
    onehot = (labels[:, None] == jnp.arange(CLASSES, dtype=jnp.int32)[None, :]).astype(jnp.float32)
    gradient = jnp.dot((probs - onehot).T, features, precision=highest, preferred_element_type=jnp.float32) / ROWS

    def operate(vector):
        tangent = jnp.dot(features, vector.T, precision=highest, preferred_element_type=jnp.float32)
        bent = probs * tangent - probs * jnp.sum(probs * tangent, axis=1, keepdims=True)
        back = jnp.dot(bent.T, features, precision=highest, preferred_element_type=jnp.float32)
        return back / ROWS + damping * vector

    solution = jnp.zeros_like(weights)
    residual = -gradient
    direction = residual
    norm_now = jnp.sum(residual * residual)
    for iteration in range(ITERS):
        image = operate(direction)
        step_size = norm_now / jnp.sum(direction * image)
        solution = solution + step_size * direction
        residual = residual - step_size * image
        norm_next = jnp.sum(residual * residual)
        direction = residual + (norm_next / norm_now) * direction
        norm_now = norm_next
    return weights + solution, residual
```

```python
import jax
import jax.numpy as jnp
from jax import lax
from jax.experimental import pallas as pl
from jax.experimental.pallas import tpu as pltpu
from jax.sharding import PartitionSpec as P

damping = 0.01

RING = 4
LANES = 128
ROW_BLOCKS = 3


class Ring:
    def __init__(self, here, left, right, sems, base):
        self.here, self.left, self.right = here, left, right
        self.send, self.recv = sems
        self.base = base

    def copy(self, slot, src, dst, to):
        return pltpu.make_async_remote_copy(
            src_ref=src,
            dst_ref=dst,
            send_sem=self.send.at[self.base + slot],
            recv_sem=self.recv.at[self.base + slot],
            device_id=to,
            device_id_type=pl.DeviceIdType.MESH,
        )


class Reduce:
    def __init__(self, ring, work, start, seg, top, from_left, from_right, base):
        self.ring, self.work, self.start, self.seg, self.top = ring, work, start, seg, top
        self.relay_l, self.last_l = from_left
        self.relay_r, self.last_r = from_right
        self.low = seg - top
        i = ring.here
        self.own, self.nxt, self.prv, self.opp = i, (i + 1) % RING, (i + 3) % RING, (i + 2) % RING
        ring.base = base
        r = ring
        self.c_relay_r = self.cp(base, 0, self.opp, 0, self.top, self.relay_l, r.right)
        self.c_relay_l = self.cp(base, 1, self.opp, self.top, self.low, self.relay_r, r.left)
        self.c_dir_r = self.cp(
            base, 2, self.nxt, self.top, self.low, self.last_l(self.top, self.low), r.right
        )
        self.c_dir_l = self.cp(base, 3, self.prv, 0, self.top, self.last_r(0, self.top), r.left)
        self.c_sum_r = self.cp(base, 4, self.nxt, 0, self.top, self.last_l(0, self.top), r.right)
        self.c_sum_l = self.cp(
            base, 5, self.prv, self.top, self.low, self.last_r(self.top, self.low), r.left
        )

    def rows(self, seg, off, size):
        return pl.ds(pl.multiple_of(self.start + seg * self.seg + off, 8), size)

    def cp(self, base, slot, seg, off, size, dst, to):
        self.ring.base = base
        if callable(dst):
            dst = dst(0, size)
        return self.ring.copy(slot, self.work.at[self.rows(seg, off, size)], dst, to)

    def first(self):
        self.c_relay_r.start()
        self.c_relay_l.start()
        self.c_dir_r.start()
        self.c_dir_l.start()

    def second(self):
        self.c_relay_r.wait_recv()
        at = self.rows(self.nxt, 0, self.top)
        self.work[at] = self.work[at] + self.relay_l(0, self.top)[...]
        self.c_sum_r.start()
        self.c_relay_l.wait_recv()
        at = self.rows(self.prv, self.top, self.low)
        self.work[at] = self.work[at] + self.relay_r(0, self.low)[...]
        self.c_sum_l.start()

    def last(self, store):
        self.c_dir_l.wait_recv()
        self.c_sum_r.wait_recv()
        store(
            0,
            self.work[self.rows(self.own, 0, self.top)]
            + (self.last_l(0, self.top)[...] + self.last_r(0, self.top)[...]),
        )
        self.c_dir_r.wait_recv()
        self.c_sum_l.wait_recv()
        store(
            self.top,
            self.work[self.rows(self.own, self.top, self.low)]
            + (self.last_l(self.top, self.low)[...] + self.last_r(self.top, self.low)[...]),
        )

    def sent(self):
        for c in (
            self.c_relay_r,
            self.c_relay_l,
            self.c_dir_r,
            self.c_dir_l,
            self.c_sum_r,
            self.c_sum_l,
        ):
            c.wait_send()


class Gather:
    def __init__(self, ring, whole, start, seg, top, base):
        self.whole, self.start, self.seg, self.top = whole, start, seg, top
        low = seg - top
        i = ring.here
        nxt, prv = (i + 1) % RING, (i + 3) % RING

        def cp(slot, s, off, size, to):
            ring.base = base
            ref = whole.at[pl.ds(pl.multiple_of(start + s * seg + off, 8), size)]
            return ring.copy(slot, ref, ref, to)

        self.r_top = cp(0, i, 0, top, ring.right)
        self.l_low = cp(1, i, top, low, ring.left)
        self.r_low = cp(2, i, top, low, ring.right)
        self.l_top = cp(3, i, 0, top, ring.left)
        self.r_on = cp(4, prv, 0, top, ring.right)
        self.l_on = cp(5, nxt, top, low, ring.left)

    def first(self):
        self.r_top.start()
        self.l_low.start()
        self.r_low.start()
        self.l_top.start()

    def second(self):
        self.r_top.wait_recv()
        self.r_on.start()
        self.l_low.wait_recv()
        self.l_on.start()

    def last(self):
        self.r_low.wait_recv()
        self.l_top.wait_recv()
        self.r_on.wait_recv()
        self.l_on.wait_recv()

    def sent(self):
        for c in (self.r_top, self.l_low, self.r_low, self.l_top, self.r_on, self.l_on):
            c.wait_send()


def up(value, unit):
    return -(-value // unit) * unit


def sizes(rows_dev, feats_dev, classes):
    blocks = feats_dev // LANES
    half = blocks // 2
    sub = up(half * classes + 8, RING * RING * 8) // (RING * RING)
    rb_rows = rows_dev // ROW_BLOCKS
    rb_blocks = rb_rows // LANES
    zseg = up(rb_blocks * classes + 16, 2 * RING * 8) // (2 * RING)
    return dict(
        blocks=blocks,
        half=half,
        sub=sub,
        seg=sub * RING,
        side=sub * RING * RING,
        rb_rows=rb_rows,
        rb_blocks=rb_blocks,
        zseg=zseg,
        zhalf=zseg * RING,
        zall=zseg * RING * 2,
    )


def tile_sum(value):
    return value.reshape(-1, 8, LANES).sum(axis=0)


def total(tile):
    return jnp.sum(jnp.sum(tile, axis=1, keepdims=True), axis=0, keepdims=True)


def split(value):
    high = value.astype(jnp.bfloat16)
    return high, (value - high.astype(jnp.float32)).astype(jnp.bfloat16)


NT = (((1,), (1,)), ((), ()))
NN = (((1,), (0,)), ((), ()))


def dot3(a_hi, a_lo, b_hi, b_lo, dims):
    def dot(a, b):
        return lax.dot_general(a, b, dims, preferred_element_type=jnp.float32)

    return dot(a_hi, b_hi) + (dot(a_lo, b_hi) + dot(a_hi, b_lo))


def make_kernel(s, rows_dev, feats_dev, classes, total_rows, stage_rows):
    blocks, half, rb_rows, rb_blocks = s["blocks"], s["half"], s["rb_rows"], s["rb_blocks"]
    seg, sub, side = s["seg"], s["sub"], s["side"]
    zseg, zhalf, zall = s["zseg"], s["zhalf"], s["zall"]
    ztop = up(zseg // 2, 8)
    subtop = up(sub // 2, 8)
    segtop = up(seg // 2, 8)

    def place(block):
        return block * classes if block < half else side + (block - half) * classes

    mark = half * classes
    zmark = rb_blocks * classes

    def kernel(
        f_hbm,
        w_hbm,
        lab_ref,
        sol_ref,
        res_ref,
        f_hi,
        f_lo,
        stage,
        d_hi,
        d_lo,
        part,
        whole,
        probs,
        tan0,
        b_hi,
        b_lo,
        zpart,
        zwhole,
        zcore,
        zrl,
        zll,
        zrr,
        zlr,
        xrl,
        xll,
        xrr,
        xlr,
        yrl,
        yll,
        yrr,
        ylr,
        load_sem,
        send_sem,
        recv_sem,
    ):
        clip, feat = lax.axis_index("clip"), lax.axis_index("feat")
        y, x = clip // RING, clip % RING
        z, core = feat // 2, feat % 2
        sems = (send_sem, recv_sem)

        x_right = (y * RING + (x + 1) % RING, feat)
        x_left = (y * RING + (x + 3) % RING, feat)
        y_right = (((y + 1) % RING) * RING + x, feat)
        y_left = (((y + 3) % RING) * RING + x, feat)
        z_right = (clip, ((z + 1) % RING) * 2 + core)
        z_left = (clip, ((z + 3) % RING) * 2 + core)
        other = (clip, z * 2 + 1 - core)

        slots = stage.shape[0]
        pieces = [(w_hbm, o, min(stage_rows, classes - o)) for o in range(0, classes, stage_rows)]
        pieces += [(f_hbm, o, stage_rows) for o in range(0, rows_dev, stage_rows)]

        def load(n):
            src, off, size = pieces[n]
            return pltpu.make_async_copy(
                src.at[pl.ds(off, size)],
                stage.at[n % slots, pl.ds(0, size)],
                load_sem.at[n % slots],
            )

        for n in range(slots):
            load(n).start()

        barrier = pltpu.get_barrier_semaphore()
        for peer in (x_left, x_right, y_left, y_right, z_left, z_right, other):
            pl.semaphore_signal(
                barrier, inc=1, device_id=peer, device_id_type=pl.DeviceIdType.MESH
            )

        part[pl.ds(mark, side - mark)] = jnp.zeros((side - mark, LANES), jnp.float32)
        part[pl.ds(side + mark, side - mark)] = jnp.zeros((side - mark, LANES), jnp.float32)
        for rb in range(ROW_BLOCKS):
            zpart[pl.ds(rb * zall + zmark, zall - zmark)] = jnp.zeros(
                (zall - zmark, LANES), jnp.float32
            )

        def take(n):
            src, off, size = pieces[n]
            load(n).wait()
            high, low = split(stage[n % slots, pl.ds(0, size)])
            if src is w_hbm:
                d_hi[pl.ds(off, size)], d_lo[pl.ds(off, size)] = high, low
            else:
                f_hi[pl.ds(off, size)], f_lo[pl.ds(off, size)] = high, low
            if n + slots < len(pieces):
                load(n + slots).start()

        def z_core(rb):
            base = rb * zall
            return pltpu.make_async_remote_copy(
                src_ref=zpart.at[pl.ds(pl.multiple_of(base + (1 - core) * zhalf, 8), zhalf)],
                dst_ref=zcore.at[pl.ds(pl.multiple_of(rb * zhalf, 8), zhalf)],
                send_sem=send_sem.at[96 + rb * 14],
                recv_sem=recv_sem.at[96 + rb * 14],
                device_id=other,
                device_id_type=pl.DeviceIdType.MESH,
            )

        def z_back(rb):
            at = pl.ds(pl.multiple_of(rb * zall + core * zhalf, 8), zhalf)
            return pltpu.make_async_remote_copy(
                src_ref=zwhole.at[at],
                dst_ref=zwhole.at[at],
                send_sem=send_sem.at[96 + rb * 14 + 13],
                recv_sem=recv_sem.at[96 + rb * 14 + 13],
                device_id=other,
                device_id_type=pl.DeviceIdType.MESH,
            )

        def forward(rb):
            rows = pl.ds(pl.multiple_of(rb * rb_rows, rb_rows), rb_rows)
            value = dot3(d_hi[...], d_lo[...], f_hi[rows], f_lo[rows], NT)
            for b in range(rb_blocks):
                zpart[pl.ds(pl.multiple_of(rb * zall + b * classes, 8), classes)] = value[
                    :, b * LANES : (b + 1) * LANES
                ]
            z_core(rb).start()

        def z_ring():
            return Ring(z, z_left, z_right, sems, 0)

        def window(ref, base):
            return lambda off, size: ref.at[pl.ds(base + off, size)]

        def sum_over_feat(finish):
            reds, gats = [], []
            for rb in range(ROW_BLOCKS):
                own = rb * zall + core * zhalf
                reds.append(
                    Reduce(
                        z_ring(),
                        zpart,
                        own,
                        zseg,
                        ztop,
                        (window(zrl, rb * ztop), window(zll, rb * zseg)),
                        (window(zrr, rb * (zseg - ztop)), window(zlr, rb * zseg)),
                        96 + rb * 14 + 1,
                    )
                )
                gats.append(Gather(z_ring(), zwhole, own, zseg, ztop, 96 + rb * 14 + 7))
            for rb in range(ROW_BLOCKS):
                z_core(rb).wait_recv()
                at = pl.ds(pl.multiple_of(rb * zall + core * zhalf, 8), zhalf)
                zpart[at] = zpart[at] + zcore[pl.ds(rb * zhalf, zhalf)]
                reds[rb].first()
            for rb in range(ROW_BLOCKS):
                reds[rb].second()
            for rb in range(ROW_BLOCKS):

                def store(off, value, rb=rb):
                    at = rb * zall + core * zhalf + z * zseg + off
                    zwhole[pl.ds(pl.multiple_of(at, 8), value.shape[0])] = value

                reds[rb].last(store)
                gats[rb].first()
            for rb in range(ROW_BLOCKS):
                gats[rb].second()
            for rb in range(ROW_BLOCKS):
                gats[rb].last()
                z_back(rb).start()
            for rb in range(ROW_BLOCKS):
                z_back(rb).wait_recv()
                finish(rb)
            for rb in range(ROW_BLOCKS):
                z_core(rb).wait_send()
                reds[rb].sent()
                gats[rb].sent()
                z_back(rb).wait_send()

        def row_sums(rb, b):
            return zwhole[pl.ds(rb * zall + b * classes, classes)]

        def row_carried(n):
            return total(zwhole[pl.ds(zmark + 8 * n, 8)])

        def keep_rows(rb, b, value):
            lanes = pl.ds((rb * rb_blocks + b) * LANES, LANES)
            b_hi[:, lanes], b_lo[:, lanes] = split(value)

        def backward(rb):
            rows = pl.ds(rb * rb_rows, rb_rows)
            a_hi, a_lo = b_hi[:, rows], b_lo[:, rows]
            for pair in range(0, blocks, 2):
                lanes = pl.ds(pair * LANES, 2 * LANES)
                value = dot3(a_hi, a_lo, f_hi[rows, lanes], f_lo[rows, lanes], NN)
                for b in range(2):
                    at = pl.ds(place(pair + b), classes)
                    new = value[:, b * LANES : (b + 1) * LANES]
                    part[at] = new if rb == 0 else part[at] + new

        def sum_over_clip(turn, scale):
            x_ring, y_ring = (x, x_left, x_right), (y, y_left, y_right)
            red1, red2, gat2, gat1 = [], [], [], []
            for q, (one, two) in enumerate(((x_ring, y_ring), (y_ring, x_ring))):
                start, base = q * side, q * 24
                own = start + one[0] * seg
                red1.append(
                    Reduce(
                        Ring(*one, sems, 0),
                        part,
                        start,
                        seg,
                        segtop,
                        (window(xrl, q * segtop), window(xll, q * seg)),
                        (window(xrr, q * (seg - segtop)), window(xlr, q * seg)),
                        base,
                    )
                )
                red2.append(
                    Reduce(
                        Ring(*two, sems, 0),
                        part,
                        own,
                        sub,
                        subtop,
                        (window(yrl, q * subtop), window(yll, q * sub)),
                        (window(yrr, q * (sub - subtop)), window(ylr, q * sub)),
                        base + 6,
                    )
                )
                gat2.append(
                    Gather(Ring(*two, sems, 0), whole.at[turn], own, sub, subtop, base + 12)
                )
                gat1.append(
                    Gather(Ring(*one, sems, 0), whole.at[turn], start, seg, segtop, base + 18)
                )
            for q in range(2):
                red1[q].first()
            for q in range(2):
                red1[q].second()
            for q in range(2):

                def keep(off, value, q=q):
                    part[red1[q].rows(red1[q].own, off, value.shape[0])] = value

                red1[q].last(keep)
                red2[q].first()
            for q in range(2):
                red2[q].second()
            for q in range(2):

                def store(off, value, q=q):
                    at = red2[q].rows(red2[q].own, off, value.shape[0])
                    whole.at[turn][at] = value * scale

                red2[q].last(store)
                gat2[q].first()
            for q in range(2):
                gat2[q].second()
            for q in range(2):
                gat2[q].last()
                gat1[q].first()
            for q in range(2):
                gat1[q].second()
            for q in range(2):
                gat1[q].last()
            for q in range(2):
                red1[q].sent()
                red2[q].sent()
                gat2[q].sent()
                gat1[q].sent()

        def feats(turn, block):
            return whole[turn, pl.ds(place(block), classes)]

        def carried(turn):
            return total(whole[turn, pl.ds(mark, 8)])

        def direct(block, value):
            lanes = pl.ds(block * LANES, LANES)
            d_hi[:, lanes], d_lo[:, lanes] = split(value)

        per_block = rb_rows // stage_rows
        w_pieces = len(pieces) - rows_dev // stage_rows
        for n in range(w_pieces):
            take(n)
        pl.semaphore_wait(barrier, 7)
        for rb in range(ROW_BLOCKS):
            for n in range(per_block):
                take(w_pieces + rb * per_block + n)
            forward(rb)

        def softmax_rows(rb):
            for b in range(rb_blocks):
                logits = row_sums(rb, b)
                grown = jnp.exp(logits - jnp.max(logits, axis=0, keepdims=True))
                prob = grown / jnp.sum(grown, axis=0, keepdims=True)
                probs[pl.ds((rb * rb_blocks + b) * classes, classes)] = prob
                which = lax.broadcasted_iota(jnp.int32, (classes, LANES), 0)
                hit = which == lab_ref[pl.ds(rb * rb_blocks + b, 1), :]
                keep_rows(rb, b, prob - jnp.where(hit, 1.0, 0.0))
            backward(rb)

        sum_over_feat(softmax_rows)
        sum_over_clip(0, -1.0 / total_rows)

        norm = jnp.zeros((8, LANES), jnp.float32)
        for block in range(blocks):
            value = feats(0, block)
            norm = norm + tile_sum(value * value)
            direct(block, value)
        zpart[pl.ds(zmark, 8)] = norm
        lax.fori_loop(0, ROW_BLOCKS, lambda rb, _: (forward(rb), 0)[1], 0)

        def bend(rb, b, tangent):
            prob = probs[pl.ds((rb * rb_blocks + b) * classes, classes)]
            weighted = prob * tangent
            bent = weighted - prob * jnp.sum(weighted, axis=0, keepdims=True)
            keep_rows(rb, b, bent)
            return tile_sum(tangent * bent)

        curve = []

        def first_rows(rb):
            for b in range(rb_blocks):
                tangent = row_sums(rb, b)
                tan0[pl.ds((rb * rb_blocks + b) * classes, classes)] = tangent
                curve.append(bend(rb, b, tangent))
            backward(rb)

        sum_over_feat(first_rows)
        norm0 = row_carried(0)
        part[pl.ds(mark, 8)] = sum(curve[1:], curve[0])
        sum_over_clip(1, 1.0 / total_rows)
        step0 = norm0 / (carried(1) + damping * norm0)

        def residual1(block):
            first = feats(0, block)
            return first, first - step0 * (feats(1, block) + damping * first)

        norm = jnp.zeros((8, LANES), jnp.float32)
        cross = jnp.zeros((8, LANES), jnp.float32)
        for block in range(blocks):
            first, value = residual1(block)
            norm = norm + tile_sum(value * value)
            cross = cross + tile_sum(value * first)
            direct(block, value)
        zpart[pl.ds(zmark, 8)] = norm
        zpart[pl.ds(zmark + 8, 8)] = cross
        lax.fori_loop(0, ROW_BLOCKS, lambda rb, _: (forward(rb), 0)[1], 0)

        curve.clear()
        scalars = {}

        def second_rows(rb):
            if rb == 0:
                scalars["norm1"] = row_carried(0)
                scalars["cross"] = row_carried(1)
                scalars["beta"] = scalars["norm1"] / norm0
            for b in range(rb_blocks):
                before = tan0[pl.ds((rb * rb_blocks + b) * classes, classes)]
                curve.append(bend(rb, b, row_sums(rb, b) + scalars["beta"] * before))
            backward(rb)

        sum_over_feat(second_rows)
        norm1, beta = scalars["norm1"], scalars["beta"]
        part[pl.ds(mark, 8)] = sum(curve[1:], curve[0])
        sum_over_clip(2, 1.0 / total_rows)
        length = norm1 + 2.0 * beta * scalars["cross"] + beta * beta * norm0
        step1 = norm1 / (carried(2) + damping * length)
        for block in range(blocks):
            first, value = residual1(block)
            direction = value + beta * first
            lanes = pl.ds(block * LANES, LANES)
            sol_ref[:, lanes] = step0 * first + step1 * direction
            res_ref[:, lanes] = step1 * (feats(2, block) + damping * direction) - value

    return kernel


def local(features, weights, labels):
    rows_dev, feats_dev = features.shape
    classes = weights.shape[0]
    total_rows = rows_dev * lax.axis_size("clip")
    s = sizes(rows_dev, feats_dev, classes)
    stage_rows = 128
    seg, sub, side = s["seg"], s["sub"], s["side"]
    zseg, zhalf, zall = s["zseg"], s["zhalf"], s["zall"]
    ztop, subtop, segtop = up(zseg // 2, 8), up(sub // 2, 8), up(seg // 2, 8)
    f32, bf16 = jnp.float32, jnp.bfloat16

    def rows(n):
        return pltpu.VMEM((n, LANES), f32)

    scratch = [
        pltpu.VMEM((rows_dev, feats_dev), bf16),
        pltpu.VMEM((rows_dev, feats_dev), bf16),
        pltpu.VMEM((3, stage_rows, feats_dev), f32),
        pltpu.VMEM((classes, feats_dev), bf16),
        pltpu.VMEM((classes, feats_dev), bf16),
        rows(2 * side),
        pltpu.VMEM((3, 2 * side, LANES), f32),
        rows(rows_dev // LANES * classes),
        rows(rows_dev // LANES * classes),
        pltpu.VMEM((classes, rows_dev), bf16),
        pltpu.VMEM((classes, rows_dev), bf16),
        rows(ROW_BLOCKS * zall),
        rows(ROW_BLOCKS * zall),
        rows(ROW_BLOCKS * zhalf),
        rows(ROW_BLOCKS * ztop),
        rows(ROW_BLOCKS * zseg),
        rows(ROW_BLOCKS * (zseg - ztop)),
        rows(ROW_BLOCKS * zseg),
        rows(2 * segtop),
        rows(2 * seg),
        rows(2 * (seg - segtop)),
        rows(2 * seg),
        rows(2 * subtop),
        rows(2 * sub),
        rows(2 * (sub - subtop)),
        rows(2 * sub),
        pltpu.SemaphoreType.DMA((3,)),
        pltpu.SemaphoreType.DMA((138,)),
        pltpu.SemaphoreType.DMA((138,)),
    ]
    moved, against = pl.pallas_call(
        make_kernel(s, rows_dev, feats_dev, classes, total_rows, stage_rows),
        name="steps",
        out_shape=[jax.ShapeDtypeStruct(weights.shape, f32)] * 2,
        in_specs=[
            pl.BlockSpec(memory_space=pl.ANY),
            pl.BlockSpec(memory_space=pl.ANY),
            pl.BlockSpec(memory_space=pltpu.VMEM),
        ],
        out_specs=[pl.BlockSpec(memory_space=pltpu.VMEM)] * 2,
        scratch_shapes=scratch,
        compiler_params=pltpu.CompilerParams(
            collective_id=0, has_side_effects=True, vmem_limit_bytes=67_000_000
        ),
    )(features, weights, labels.reshape(rows_dev // LANES, LANES))
    return weights + moved, -against


def solution(mesh):
    in_specs = (P("clip", "feat"), P(None, "feat"), P("clip"))
    out_specs = (P(None, "feat"), P(None, "feat"))
    return jax.shard_map(local, mesh=mesh, in_specs=in_specs, out_specs=out_specs, check_vma=False)
```

```python
import jax
import jax.numpy as jnp
from jax import lax
from jax.experimental import pallas as pl
from jax.experimental.pallas import tpu as pltpu
from jax.sharding import PartitionSpec as P

damping = 0.01

RING = 4
LANES = 128
ROW_BLOCKS = 3
TURNS = 3
STAGE = 128
SLOTS = 4
NT = (((1,), (1,)), ((), ()))
NN = (((1,), (0,)), ((), ()))


def up(value, unit):
    return -(-value // unit) * unit


def at(start, size):
    return pl.ds(start if isinstance(start, int) else pl.multiple_of(start, 8), size)


class Sems:
    def __init__(self, send, recv):
        self.send, self.recv, self.used = send, recv, 0

    def copy(self, src, dst, to):
        n = self.used
        self.used += 1
        return pltpu.make_async_remote_copy(
            src_ref=src,
            dst_ref=dst,
            send_sem=self.send.at[n],
            recv_sem=self.recv.at[n],
            device_id=to,
            device_id_type=pl.DeviceIdType.MESH,
        )


class Reduce:
    def __init__(self, sems, ring, work, start, seg, land, land_at):
        here, left, right = ring
        top = up(seg // 2, 8)
        low = seg - top
        self.work, self.start, self.seg, self.top, self.low = work, start, seg, top, low
        self.own, self.nxt, self.prv, opp = here, (here + 1) % 4, (here + 3) % 4, (here + 2) % 4
        self.relay_l = land.at[pl.ds(land_at, top)]
        self.relay_r = land.at[pl.ds(land_at + top, low)]
        l_top = land.at[pl.ds(land_at + seg, top)]
        l_low = land.at[pl.ds(land_at + seg + top, low)]
        r_top = land.at[pl.ds(land_at + 2 * seg, top)]
        r_low = land.at[pl.ds(land_at + 2 * seg + top, low)]
        self.landed = ((l_top, r_top), (l_low, r_low))

        def cp(s, off, size, dst, to):
            return sems.copy(work.at[self.rows(s, off, size)], dst, to)

        self.go_r = cp(opp, 0, top, self.relay_l, right)
        self.go_l = cp(opp, top, low, self.relay_r, left)
        self.near_r = cp(self.nxt, top, low, l_low, right)
        self.near_l = cp(self.prv, 0, top, r_top, left)
        self.sum_r = cp(self.nxt, 0, top, l_top, right)
        self.sum_l = cp(self.prv, top, low, r_low, left)

    def rows(self, s, off, size):
        return at(self.start + s * self.seg + off, size)

    def first(self):
        self.go_r.start()
        self.go_l.start()

    def near(self, wait):
        if wait:
            self.go_r.wait_send()
            self.go_l.wait_send()
        self.near_r.start()
        self.near_l.start()

    def second(self):
        self.go_r.wait_recv()
        rows = self.rows(self.nxt, 0, self.top)
        self.work[rows] = self.work[rows] + self.relay_l[...]
        self.sum_r.start()
        self.go_l.wait_recv()
        rows = self.rows(self.prv, self.top, self.low)
        self.work[rows] = self.work[rows] + self.relay_r[...]
        self.sum_l.start()

    def last(self, store):
        self.near_l.wait_recv()
        self.sum_r.wait_recv()
        a, b = self.landed[0]
        rows = self.rows(self.own, 0, self.top)
        store(rows, self.work[rows] + (a[...] + b[...]))
        self.near_r.wait_recv()
        self.sum_l.wait_recv()
        a, b = self.landed[1]
        rows = self.rows(self.own, self.top, self.low)
        store(rows, self.work[rows] + (a[...] + b[...]))

    def sent(self, waited):
        for c in (self.near_r, self.near_l, self.sum_r, self.sum_l) + (
            () if waited else (self.go_r, self.go_l)
        ):
            c.wait_send()


class Gather:
    def __init__(self, sems, ring, whole, start, seg):
        here, left, right = ring
        top = up(seg // 2, 8)
        low = seg - top
        nxt, prv = (here + 1) % 4, (here + 3) % 4

        def cp(s, off, size, to):
            ref = whole.at[at(start + s * seg + off, size)]
            return sems.copy(ref, ref, to)

        self.go_r = cp(here, 0, top, right)
        self.go_l = cp(here, top, low, left)
        self.near_r = cp(here, top, low, right)
        self.near_l = cp(here, 0, top, left)
        self.on_r = cp(prv, 0, top, right)
        self.on_l = cp(nxt, top, low, left)

    def first(self):
        self.go_r.start()
        self.go_l.start()

    def near(self, wait):
        if wait:
            self.go_r.wait_send()
            self.go_l.wait_send()
        self.near_r.start()
        self.near_l.start()

    def second(self):
        self.go_r.wait_recv()
        self.on_r.start()
        self.go_l.wait_recv()
        self.on_l.start()

    def last(self):
        self.near_r.wait_recv()
        self.near_l.wait_recv()
        self.on_r.wait_recv()
        self.on_l.wait_recv()

    def sent(self, waited):
        for c in (self.near_r, self.near_l, self.on_r, self.on_l) + (
            () if waited else (self.go_r, self.go_l)
        ):
            c.wait_send()


def tile_sum(value):
    return value.reshape(-1, 8, LANES).sum(axis=0)


def total(tile):
    return jnp.sum(jnp.sum(tile, axis=1, keepdims=True), axis=0, keepdims=True)


def split(value):
    high = value.astype(jnp.bfloat16)
    return high, (value - high.astype(jnp.float32)).astype(jnp.bfloat16)


def dot3(stack, size, right_hi, right_lo, dims):
    def dot(a, b):
        return lax.dot_general(a, b, dims, preferred_element_type=jnp.float32)

    both = dot(stack, right_hi)
    return both[:size] + (both[size:] + dot(stack[:size], right_lo))


class Sizes:
    def __init__(self, rows_dev, feats_dev, classes):
        first = up(classes // 2, 16)
        self.chunks = (first, classes - first)
        self.offs = (0, first)
        self.blocks = feats_dev // LANES
        self.row_lanes = rows_dev // LANES
        self.rb_rows = rows_dev // ROW_BLOCKS
        self.rb_blocks = self.rb_rows // LANES
        self.sub = [up(self.blocks * c + 8, 2 * 16 * 8) // 32 for c in self.chunks]
        self.seg = [s * RING for s in self.sub]
        self.side = [s * RING for s in self.seg]
        self.mark = [self.blocks * c for c in self.chunks]
        self.zmark = [self.rb_blocks * c for c in self.chunks]
        self.zseg = [up(m + 16, 2 * RING * 8) // (2 * RING) for m in self.zmark]
        self.zhalf = [s * RING for s in self.zseg]
        self.zall = [s * 2 for s in self.zhalf]


def make_kernel(s, rows_dev, classes, total_rows):
    def kernel(f_hbm, w_hbm, lab_ref, sol_hbm, res_hbm, f_hi, f_lo, stage, *rest):
        d, part, whole, probs, tan0, b_, zpart, zwhole, zcore, zland, land, outs = (
            rest[2 * n : 2 * n + 2] for n in range(12)
        )
        load_sem, out_sem, send_sem, recv_sem, zsend_sem, zrecv_sem = rest[24:]
        clip, feat = lax.axis_index("clip"), lax.axis_index("feat")
        y, x = clip // RING, clip % RING
        z, core = feat // 2, feat % 2

        def at_x(step):
            return (y * RING + (x + step) % RING, feat)

        def at_y(step):
            return (((y + step) % RING) * RING + x, feat)

        def at_z(step):
            return (clip, ((z + step) % RING) * 2 + core)

        other = (clip, z * 2 + 1 - core)
        x_ring, y_ring = (x, at_x(3), at_x(1)), (y, at_y(3), at_y(1))

        w_pieces = []
        for c in range(2):
            top = up(s.chunks[c] // 2, 16)
            w_pieces += [(c, 0, top), (c, top, s.chunks[c] - top)]

        def load_w(n):
            c, off, size = w_pieces[n]
            return pltpu.make_async_copy(
                w_hbm.at[pl.ds(s.offs[c] + off, size)],
                stage.at[n, pl.ds(0, size)],
                load_sem.at[n],
            )

        def load_f(n, slot):
            return pltpu.make_async_copy(
                f_hbm.at[at(n * STAGE, STAGE)], stage.at[slot], load_sem.at[slot]
            )

        for n in range(SLOTS):
            load_w(n).start()
        peers = [at_x(1), at_x(3), at_y(1), at_y(3), at_z(1), at_z(2), at_z(3), other]
        barrier = pltpu.get_barrier_semaphore()
        for peer in peers:
            pl.semaphore_signal(
                barrier, inc=1, device_id=peer, device_id_type=pl.DeviceIdType.MESH
            )

        for c in range(2):
            pad = 2 * s.side[c] - s.mark[c]
            part[c][pl.ds(s.mark[c], pad)] = jnp.zeros((pad, LANES), jnp.float32)
            pad = s.zall[c] - s.zmark[c]
            for rb in range(ROW_BLOCKS):
                zpart[c][pl.ds(rb * s.zall[c] + s.zmark[c], pad)] = jnp.zeros(
                    (pad, LANES), jnp.float32
                )

        def z_copy(c, rb, n, src, dst, to):
            sem = (c * ROW_BLOCKS + rb) * 8 + n
            return pltpu.make_async_remote_copy(
                src_ref=src,
                dst_ref=dst,
                send_sem=zsend_sem.at[sem],
                recv_sem=zrecv_sem.at[sem],
                device_id=to,
                device_id_type=pl.DeviceIdType.MESH,
            )

        def z_own(c, rb):
            return rb * s.zall[c] + core * s.zhalf[c]

        def z_core(c, rb):
            half = s.zhalf[c]
            src = zpart[c].at[at(rb * s.zall[c] + (1 - core) * half, half)]
            return z_copy(c, rb, 0, src, zcore[c].at[at(rb * half, half)], other)

        def z_land(c, rb, step):
            return zland[c].at[at((rb * 3 + step - 1) * s.zseg[c], s.zseg[c])]

        def z_out(c, rb, step):
            src = zpart[c].at[at(z_own(c, rb) + (z + step) % RING * s.zseg[c], s.zseg[c])]
            return z_copy(c, rb, step, src, z_land(c, rb, step), at_z(step))

        def z_mine(c, rb):
            return at(z_own(c, rb) + z * s.zseg[c], s.zseg[c])

        def z_all(c, rb, step):
            ref = zwhole[c].at[z_mine(c, rb)]
            return z_copy(c, rb, 3 + step, ref, ref, at_z(step))

        def z_back(c, rb):
            ref = zwhole[c].at[at(z_own(c, rb), s.zhalf[c])]
            return z_copy(c, rb, 7, ref, ref, other)

        def forward(c, rb):
            rows = pl.ds(pl.multiple_of(rb * s.rb_rows, s.rb_rows), s.rb_rows)
            value = dot3(d[c][...], s.chunks[c], f_hi[rows], f_lo[rows], NT)
            for b in range(s.rb_blocks):
                zpart[c][at(rb * s.zall[c] + b * s.chunks[c], s.chunks[c])] = value[
                    :, b * LANES : (b + 1) * LANES
                ]
            z_core(c, rb).start()

        def forwards(c):
            lax.fori_loop(0, ROW_BLOCKS, lambda rb, _: (forward(c, rb), 0)[1], 0)

        def z_step1(c):
            for rb in range(ROW_BLOCKS):
                z_core(c, rb).wait_recv()
                rows = at(z_own(c, rb), s.zhalf[c])
                zpart[c][rows] = zpart[c][rows] + zcore[c][at(rb * s.zhalf[c], s.zhalf[c])]
                for step in (2, 1, 3):
                    z_out(c, rb, step).start()

        def z_step2(c):
            for rb in range(ROW_BLOCKS):
                for step in (1, 2, 3):
                    z_out(c, rb, step).wait_recv()
                rows = z_mine(c, rb)
                one, two, three = (z_land(c, rb, step)[...] for step in (1, 2, 3))
                zwhole[c][rows] = (zpart[c][rows] + one) + (two + three)
                for step in (2, 1, 3):
                    z_all(c, rb, step).start()

        def z_step3(c):
            for rb in range(ROW_BLOCKS):
                for step in (1, 2, 3):
                    z_all(c, rb, step).wait_recv()
                z_back(c, rb).start()

        def z_sent(c):
            for rb in range(ROW_BLOCKS):
                z_core(c, rb).wait_send()
                for step in (1, 2, 3):
                    z_out(c, rb, step).wait_send()
                    z_all(c, rb, step).wait_send()
                z_back(c, rb).wait_send()

        def row_carried(n):
            return total(zwhole[1][pl.ds(s.zmark[1] + 8 * n, 8)])

        def lane_block(c, lb):
            return at(lb * s.chunks[c], s.chunks[c])

        def backward_block(c, rows, new):
            stack = b_[c][:, rows]
            for pair in range(0, s.blocks, 2):
                lanes = pl.ds(pair * LANES, 2 * LANES)
                value = dot3(stack, s.chunks[c], f_hi[rows, lanes], f_lo[rows, lanes], NN)
                for b in range(2):
                    to = lane_block(c, pair + b)
                    term = value[:, b * LANES : (b + 1) * LANES]
                    part[c][to] = term if new is True else jnp.where(new, term, part[c][to] + term)

        def finish(work):
            def body(rb, curve):
                for c in range(2):
                    z_back(c, rb).wait_recv()
                for b in range(s.rb_blocks):
                    sums = [
                        zwhole[c][at(rb * s.zall[c] + b * s.chunks[c], s.chunks[c])]
                        for c in range(2)
                    ]
                    lb = rb * s.rb_blocks + b
                    values, tile = work(lb, sums)
                    curve = curve + tile
                    lanes = pl.ds(pl.multiple_of(lb * LANES, LANES), LANES)
                    for c in range(2):
                        high, low = split(values[c])
                        b_[c][pl.ds(0, s.chunks[c]), lanes] = high
                        b_[c][pl.ds(s.chunks[c], s.chunks[c]), lanes] = low
                rows = pl.ds(pl.multiple_of(rb * s.rb_rows, s.rb_rows), s.rb_rows)
                backward_block(0, rows, rb == 0)
                return curve

            return lax.fori_loop(0, ROW_BLOCKS, body, jnp.zeros((8, LANES), jnp.float32))

        class Clip:
            def __init__(self, sems, c, turn, scale):
                self.red1, self.red2, self.gat2, self.gat1 = [], [], [], []
                self.c, self.turn, self.scale = c, turn, scale
                for q, (one, two) in enumerate(((x_ring, y_ring), (y_ring, x_ring))):
                    start, seg, sub = q * s.side[c], s.seg[c], s.sub[c]
                    own = start + one[0] * seg
                    place = q * 3 * (seg + sub)
                    self.red1.append(Reduce(sems, one, part[c], start, seg, land[c], place))
                    self.red2.append(
                        Reduce(sems, two, part[c], own, sub, land[c], place + 3 * seg)
                    )
                    self.gat2.append(Gather(sems, two, whole[c].at[turn], own, sub))
                    self.gat1.append(Gather(sems, one, whole[c].at[turn], start, seg))

            def keep(self, rows, value):
                part[self.c][rows] = value

            def store(self, rows, value):
                whole[self.c].at[self.turn][rows] = value * self.scale

            def r1_first(self):
                for r in self.red1:
                    r.first()

            def r1_near(self):
                for r in self.red1:
                    r.near(True)

            def r1_second(self):
                for r in self.red1:
                    r.second()

            def r1_last(self):
                for r, n in zip(self.red1, self.red2):
                    r.last(self.keep)
                    n.first()
                    n.near(False)

            def r2_second(self):
                for r in self.red2:
                    r.second()

            def r2_last(self):
                for r, n in zip(self.red2, self.gat2):
                    r.last(self.store)
                    n.first()
                    n.near(False)

            def g2_second(self):
                for r in self.gat2:
                    r.second()

            def g2_last(self):
                for r, n in zip(self.gat2, self.gat1):
                    r.last()
                    n.first()

            def g1_near(self):
                for r in self.gat1:
                    r.near(True)

            def g1_second(self):
                for r in self.gat1:
                    r.second()

            def g1_last(self):
                for r in self.gat1:
                    r.last()

            def sent(self):
                for q in range(2):
                    self.red1[q].sent(True)
                    self.red2[q].sent(False)
                    self.gat2[q].sent(False)
                    self.gat1[q].sent(True)

        def sum_over_clip(turn, scale, ready0):
            sems = Sems(send_sem, recv_sem)
            zero, one = Clip(sems, 0, turn, scale), Clip(sems, 1, turn, scale)
            zero.r1_first()
            backward_block(1, pl.ds(0, rows_dev), True)
            zero.r1_near()
            zero.r1_second()
            one.r1_first()
            zero.r1_last()
            one.r1_near()
            one.r1_second()
            zero.r2_second()
            zero.r2_last()
            one.r1_last()
            zero.g2_second()
            one.r2_second()
            zero.g2_last()
            one.r2_last()
            zero.g1_near()
            one.g2_second()
            zero.g1_second()
            one.g2_last()
            zero.g1_last()
            one.g1_near()
            ready0()
            one.g1_second()
            return zero, one

        def sum_over_feat_0():
            z_step1(0)
            z_step2(0)

        def sum_over_feat_1():
            forwards(1)
            z_step3(0)
            z_step1(1)
            z_step2(1)
            z_step3(1)

        def feats(c, turn, block):
            return whole[c][turn, lane_block(c, block)]

        def carried(turn):
            return total(whole[0][turn, pl.ds(s.mark[0], 8)])

        def direct(c, block, value):
            lanes = pl.ds(block * LANES, LANES)
            high, low = split(value)
            d[c][pl.ds(0, s.chunks[c]), lanes] = high
            d[c][pl.ds(s.chunks[c], s.chunks[c]), lanes] = low

        for n in range(SLOTS):
            load_w(n).wait()
            c, off, size = w_pieces[n]
            high, low = split(stage[n, pl.ds(0, size)])
            d[c][pl.ds(off, size)], d[c][pl.ds(s.chunks[c] + off, size)] = high, low
            load_f(n, n).start()
        pl.semaphore_wait(barrier, len(peers))

        def logits_rows(rb, _):
            for n in range(2):
                piece = 2 * rb + n
                slot = piece % SLOTS
                load_f(piece, slot).wait()
                rows = at(piece * STAGE, STAGE)
                f_hi[rows], f_lo[rows] = split(stage[slot])

                @pl.when(rb == 0)
                def _():
                    load_f(SLOTS + n, n).start()

            forward(0, rb)
            forward(1, rb)
            return 0

        lax.fori_loop(0, ROW_BLOCKS, logits_rows, 0)
        for c in range(2):
            z_step1(c)
        for c in range(2):
            z_step2(c)
        for c in range(2):
            z_step3(c)

        def softmax_rows(lb, sums):
            top = jnp.maximum(
                jnp.max(sums[0], axis=0, keepdims=True), jnp.max(sums[1], axis=0, keepdims=True)
            )
            grown = [jnp.exp(v - top) for v in sums]
            scale = jnp.sum(grown[0], axis=0, keepdims=True) + jnp.sum(
                grown[1], axis=0, keepdims=True
            )
            hit = lab_ref[pl.ds(lb, 1), :]
            values = []
            for c in range(2):
                prob = grown[c] / scale
                probs[c][lane_block(c, lb)] = prob
                which = lax.broadcasted_iota(jnp.int32, (s.chunks[c], LANES), 0) + s.offs[c]
                values.append(prob - jnp.where(which == hit, 1.0, 0.0))
            return values, jnp.zeros((8, LANES), jnp.float32)

        finish(softmax_rows)
        for c in range(2):
            z_sent(c)

        def negated(c):
            norm = jnp.zeros((8, LANES), jnp.float32)
            for block in range(s.blocks):
                value = feats(c, 0, block)
                norm = norm + tile_sum(value * value)
                direct(c, block, value)
            return norm

        norms = []

        def ready0():
            norms.append(negated(0))
            forwards(0)

        zero, one = sum_over_clip(0, -1.0 / total_rows, ready0)
        sum_over_feat_0()
        one.g1_last()
        zpart[1][pl.ds(s.zmark[1], 8)] = norms[0] + negated(1)
        sum_over_feat_1()
        zero.sent()
        one.sent()

        def bend(lb, tangents):
            prob = [probs[c][lane_block(c, lb)] for c in range(2)]
            weighted = [p * t for p, t in zip(prob, tangents)]
            mean = jnp.sum(weighted[0], axis=0, keepdims=True) + jnp.sum(
                weighted[1], axis=0, keepdims=True
            )
            bent = [w - p * mean for w, p in zip(weighted, prob)]
            return bent, tile_sum(bent[0] * tangents[0]) + tile_sum(bent[1] * tangents[1])

        def first_rows(lb, sums):
            for c in range(2):
                tan0[c][lane_block(c, lb)] = sums[c]
            return bend(lb, sums)

        part[0][pl.ds(s.mark[0], 8)] = finish(first_rows)
        for c in range(2):
            z_sent(c)
        norm0 = row_carried(0)

        def residual1(c, block, step0):
            first = feats(c, 0, block)
            return first, first - step0 * (feats(c, 1, block) + damping * first)

        def first_step():
            return norm0 / (carried(1) + damping * norm0)

        def stepped(c):
            step0 = first_step()
            norm = jnp.zeros((8, LANES), jnp.float32)
            cross = jnp.zeros((8, LANES), jnp.float32)
            for block in range(s.blocks):
                first, value = residual1(c, block, step0)
                norm = norm + tile_sum(value * value)
                cross = cross + tile_sum(value * first)
                direct(c, block, value)
            return norm, cross

        def ready1():
            norms[:] = stepped(0)
            forwards(0)

        zero, one = sum_over_clip(1, 1.0 / total_rows, ready1)
        sum_over_feat_0()
        one.g1_last()
        norm, cross = stepped(1)
        zpart[1][pl.ds(s.zmark[1], 8)] = norms[0] + norm
        zpart[1][pl.ds(s.zmark[1] + 8, 8)] = norms[1] + cross
        sum_over_feat_1()
        zero.sent()
        one.sent()

        def second_rows(lb, sums):
            beta = row_carried(0) / norm0
            return bend(
                lb, [sums[c] + beta * tan0[c][lane_block(c, lb)] for c in range(2)]
            )

        part[0][pl.ds(s.mark[0], 8)] = finish(second_rows)
        for c in range(2):
            z_sent(c)

        def out_copies(c):
            return [
                pltpu.make_async_copy(
                    outs[n].at[pl.ds(s.offs[c], s.chunks[c])],
                    (sol_hbm, res_hbm)[n].at[pl.ds(s.offs[c], s.chunks[c])],
                    out_sem.at[2 * c + n],
                )
                for n in range(2)
            ]

        def results(c):
            norm1 = row_carried(0)
            beta = norm1 / norm0
            length = norm1 + 2.0 * beta * row_carried(1) + beta * beta * norm0
            step0 = first_step()
            step1 = norm1 / (carried(2) + damping * length)
            rows = pl.ds(s.offs[c], s.chunks[c])
            for block in range(s.blocks):
                first, value = residual1(c, block, step0)
                direction = value + beta * first
                lanes = pl.ds(block * LANES, LANES)
                outs[0][rows, lanes] = step0 * first + step1 * direction
                outs[1][rows, lanes] = step1 * (feats(c, 2, block) + damping * direction) - value
            for copy in out_copies(c):
                copy.start()

        zero, one = sum_over_clip(2, 1.0 / total_rows, lambda: results(0))
        one.g1_last()
        results(1)
        zero.sent()
        one.sent()
        for c in range(2):
            for copy in out_copies(c):
                copy.wait()

    return kernel


def local(features, weights, labels):
    rows_dev, feats_dev = features.shape
    classes = weights.shape[0]
    total_rows = rows_dev * lax.axis_size("clip")
    s = Sizes(rows_dev, feats_dev, classes)
    f32, bf16 = jnp.float32, jnp.bfloat16

    def rows(n):
        return pltpu.VMEM((n, LANES), f32)

    def each(make):
        return [make(0), make(1)]

    scratch = [
        pltpu.VMEM((rows_dev, feats_dev), bf16),
        pltpu.VMEM((rows_dev, feats_dev), bf16),
        pltpu.VMEM((SLOTS, STAGE, feats_dev), f32),
        *each(lambda c: pltpu.VMEM((2 * s.chunks[c], feats_dev), bf16)),
        *each(lambda c: rows(2 * s.side[c])),
        *each(lambda c: pltpu.VMEM((TURNS, 2 * s.side[c], LANES), f32)),
        *each(lambda c: rows(s.row_lanes * s.chunks[c])),
        *each(lambda c: rows(s.row_lanes * s.chunks[c])),
        *each(lambda c: pltpu.VMEM((2 * s.chunks[c], rows_dev), bf16)),
        *each(lambda c: rows(ROW_BLOCKS * s.zall[c])),
        *each(lambda c: rows(ROW_BLOCKS * s.zall[c])),
        *each(lambda c: rows(ROW_BLOCKS * s.zhalf[c])),
        *each(lambda c: rows(ROW_BLOCKS * 3 * s.zseg[c])),
        *each(lambda c: rows(2 * 3 * (s.seg[c] + s.sub[c]))),
        *each(lambda c: pltpu.VMEM((classes, feats_dev), f32)),
        pltpu.SemaphoreType.DMA((SLOTS,)),
        pltpu.SemaphoreType.DMA((4,)),
        pltpu.SemaphoreType.DMA((96,)),
        pltpu.SemaphoreType.DMA((96,)),
        pltpu.SemaphoreType.DMA((48,)),
        pltpu.SemaphoreType.DMA((48,)),
    ]
    moved, against = pl.pallas_call(
        make_kernel(s, rows_dev, classes, total_rows),
        name="steps",
        out_shape=[jax.ShapeDtypeStruct(weights.shape, f32)] * 2,
        in_specs=[
            pl.BlockSpec(memory_space=pl.ANY),
            pl.BlockSpec(memory_space=pl.ANY),
            pl.BlockSpec(memory_space=pltpu.VMEM),
        ],
        out_specs=[pl.BlockSpec(memory_space=pl.ANY)] * 2,
        scratch_shapes=scratch,
        compiler_params=pltpu.CompilerParams(
            collective_id=0, has_side_effects=True, vmem_limit_bytes=67_000_000
        ),
    )(features, weights, labels.reshape(s.row_lanes, LANES))
    return weights + moved, -against


def solution(mesh):
    in_specs = (P("clip", "feat"), P(None, "feat"), P("clip"))
    out_specs = (P(None, "feat"), P(None, "feat"))
    return jax.shard_map(local, mesh=mesh, in_specs=in_specs, out_specs=out_specs, check_vma=False)
```
